32 devices in a mesh: store: 8 (over y, x, core), tp: 4 (over z).
Axes of the slice: x: 2, y: 2, z: 4, core: 2. Of those that a mesh axis runs over, the one named last changes fastest.
Arguments:
- hidden: bfloat16 [8, 576, 8192], P('store', None, 'tp'), may hold values from -300 to 300
- w_query: bfloat16 [8192, 4096], P(None, 'tp'), may hold values from -0.0625 to 0.0625
- w_keyvalue: bfloat16 [8192, 1024], P('tp'), may hold values from -0.1875 to 0.1875
- passage_cache: bfloat16 [32, 4, 384, 256], P('store'), may hold values from -400 to 400
- passage_ids: int32 [8, 8], replicated, may hold values from 0 to 31, as said below
- select_index: int32 [8, 576], P('store'), may hold values from 0 to 3071, as said below
- select_count: int32 [8], P('store'), may hold values from 288 to 576, as said below
Outputs:
- context: bfloat16 [8, 576, 4096], P('store', None, 'tp')
The draws below stay inside these ranges and needn't reach their ends.
Inputs may be any that keep to these rules, and one draw needn't show every extreme that they name: `passage_ids`: the passages of one prompt lie in distinct shards of the pool, shard = id // 4. `select_index`: all entries of a row are distinct positions of the prompt; the first select_count[p] of row p are in increasing order, the others are ignored. `select_count`: some prompt of every draw has 576 selected tokens.
All inputs are finite; a program needn't handle non-finite values.
Results may differ from the reference program's by a relative error of at most 0.04.
Values may be sent and summed in bfloat16 or wider, within the bound.
No kernel may reach another device: no remote copies, remote signals or barrier semaphores. Data moves between devices by JAX's collectives and lax.ppermute only.
A program may use at most 128 MiB of HBM per device.

```python
import math
import jax
import jax.numpy as jnp
from jax import lax

D = 8192
HEADS = 32
KV_HEADS = 4
HEAD_DIM = 128
PASSAGE = 384
PASSAGES = 8
ROWS = 576
POOL_DEV = 4
SEQ = 3072
PROMPTS = 8
POOL = 32


def draw_hidden(key, part):
    split = jax.random.split(jax.random.fold_in(key, 11), 3)
    noise = jnp.clip(jax.random.normal(split[0], (PROMPTS, ROWS, D), jnp.float32), -4.0, 4.0)
    row_scale = jnp.exp(jax.random.uniform(split[1], (PROMPTS, ROWS, 1), jnp.float32, 0.0, math.log(10.0)))
    column_scale = jnp.exp(jax.random.uniform(split[2], (D,), jnp.float32, math.log(0.5), math.log(5.0)))
    return (noise * row_scale * column_scale).astype(jnp.bfloat16)


def draw_passage_cache(key, part):
    split = jax.random.split(jax.random.fold_in(key, 13), 1)
    shape = (POOL, KV_HEADS, PASSAGE, 2 * HEAD_DIM)
    result = 2.0 * jnp.clip(jax.random.normal(split[0], shape, jnp.float32), -4.0, 4.0)
    return result.astype(jnp.bfloat16)


def owner_draw(subkey):
    return jax.random.permutation(subkey, PROMPTS)[:PASSAGES]


def draw_passage_ids(key, part):
    split = jax.random.split(jax.random.fold_in(key, 17), 3)
    owners = jax.vmap(owner_draw)(jax.random.split(split[0], PROMPTS)).astype(jnp.int32)
    first_pick = jax.random.randint(split[1], (PROMPTS, PASSAGES), 0, POOL_DEV)
    second_pick = jax.random.randint(split[2], (PROMPTS, PASSAGES), 0, POOL_DEV)
    local_index = jnp.minimum(first_pick, second_pick)
    return (owners * POOL_DEV + local_index).astype(jnp.int32)


def selection(key):
    split = jax.random.split(jax.random.fold_in(key, 19), 3)
    counts = jax.random.randint(split[0], (PROMPTS,), ROWS // 2, ROWS + 1)
    fullest = jax.random.randint(split[1], (), 0, PROMPTS)
    counts = jnp.where(jnp.arange(PROMPTS) == fullest, ROWS, counts).astype(jnp.int32)
    ranking = jax.random.randint(split[2], (PROMPTS, SEQ), 0, 2 ** 30 // SEQ) * SEQ + jnp.arange(SEQ)
    picked = lax.top_k(ranking, ROWS)[1].astype(jnp.int32)
    order_key = jnp.where(jnp.arange(ROWS)[None, :] < counts[:, None], picked, picked + SEQ)
    ordered = jnp.sort(order_key, axis=1)
    positions = jnp.where(ordered >= SEQ, ordered - SEQ, ordered)
    return (counts, positions.astype(jnp.int32))


def draw_select_index(key, part):
    return selection(key)[1]


def draw_select_count(key, part):
    return selection(key)[0]


def raised(drawn, rng, source, target, blocks, factor):
    owner, partner = [(jnp.arange(drawn.shape[position]) // (drawn.shape[position] // blocks)).reshape([-1 if axis == position else 1 for axis in range(drawn.ndim)]) for position in (source, target)]
    chosen = jax.random.permutation(rng, blocks)[partner]
    strong = (owner == chosen) | (owner == (partner + blocks // 2) % blocks)
    return jnp.where(strong, factor * drawn, drawn)


def block_levels(rng, shape, cuts, low, largest):
    loudness = 1.0
    for position, parts in cuts:
        draws = jax.random.uniform(jax.random.fold_in(jax.random.fold_in(rng, 6), position), (parts,), jnp.float32, low / len(cuts), largest / len(cuts))
        loudness = loudness * jnp.repeat(jnp.exp(draws), shape[position] // parts).reshape((-1,) + (1,) * (len(shape) - 1 - position))
    return loudness


def gaussian(stream_key, extent, scale, most, cuts=(), kind=jnp.bfloat16):
    values = scale * jax.random.normal(stream_key, extent, jnp.float32)
    if cuts:
        values = values * block_levels(stream_key, extent, cuts, -0.22, 0.18)
    return jnp.clip(values, -most, most).astype(kind)


def gaussian_with(own_key, dims, width, limit, cuts, heavy, held_as=jnp.bfloat16):
    entries = width * jax.random.normal(own_key, dims, jnp.float32)
    if cuts:
        entries = entries * block_levels(own_key, dims, cuts, -0.22, 0.18)
    return jnp.clip(raised(entries, jax.random.fold_in(own_key, 3), *heavy), -limit, limit).astype(held_as)


def setup_inputs(seed: int = 0) -> dict:
    seeds = jax.random.split(jax.random.key(seed), 8)
    hidden = draw_hidden(jax.random.fold_in(seeds[7], 71), 0)
    w_query = gaussian(seeds[1], (D, HEADS * HEAD_DIM), D ** -0.5, 0.0625, ((1, 4),))
    w_keyvalue = gaussian_with(seeds[2], (D, KV_HEADS * 2 * HEAD_DIM), (D // 4) ** -0.5, 0.1875, ((0, 4),), (0, 1, 4, 2.0))
    passage_cache = draw_passage_cache(jax.random.fold_in(seeds[7], 71), 0)
    passage_ids = draw_passage_ids(jax.random.fold_in(seeds[7], 71), 0)
    select_index = draw_select_index(jax.random.fold_in(seeds[7], 71), 0)
    select_count = draw_select_count(jax.random.fold_in(seeds[7], 71), 0)
    return dict(hidden=hidden, w_query=w_query, w_keyvalue=w_keyvalue, passage_cache=passage_cache, passage_ids=passage_ids, select_index=select_index, select_count=select_count)


ROPE_BASE = 1000000.0
EPSILON = 1e-06

def rotate(vectors, positions):
    half_dim = vectors.shape[-1] // 2
    frequency = ROPE_BASE ** (-(jnp.arange(half_dim, dtype=jnp.float32) * 2.0) / vectors.shape[-1])
    angles = positions.astype(jnp.float32)[..., None] * frequency
    cosine = jnp.cos(angles)
    sine_part = jnp.sin(angles)
    front_half = vectors[..., :half_dim]
    back_half = vectors[..., half_dim:]
    return jnp.concatenate([front_half * cosine - back_half * sine_part, back_half * cosine + front_half * sine_part], axis=-1)

def reference(hidden, w_query, w_keyvalue, passage_cache, passage_ids, select_index, select_count):
    group_size = HEADS // KV_HEADS

    def one_prompt(inputs):
        token_rows, block_list, positions, live_count = inputs
        proj_q = jnp.dot(token_rows, w_query, preferred_element_type=jnp.float32)
        proj_kv = jnp.dot(token_rows, w_keyvalue, preferred_element_type=jnp.float32)
        widened = token_rows.astype(jnp.float32)
        inverse_rms = lax.rsqrt(lax.optimization_barrier(jnp.mean(widened * widened, axis=-1)) + EPSILON)
        queries = rotate((proj_q * inverse_rms[:, None]).reshape(ROWS, HEADS, HEAD_DIM), positions[:, None])
        queries = (queries * HEAD_DIM ** (-0.5)).astype(jnp.bfloat16)
        key_value = (proj_kv * inverse_rms[:, None]).reshape(ROWS, KV_HEADS, 2 * HEAD_DIM)
        new_keys = rotate(key_value[..., :HEAD_DIM], positions[:, None]).astype(jnp.bfloat16)
        new_values = key_value[..., HEAD_DIM:].astype(jnp.bfloat16)
        stored = jnp.take(passage_cache, block_list, axis=0)
        offsets = (jnp.arange(PASSAGES) * PASSAGE).astype(jnp.int32)
        old_keys = rotate(stored[..., :HEAD_DIM].astype(jnp.float32), offsets[:, None, None]).astype(jnp.bfloat16)
        old_keys = jnp.transpose(old_keys, (0, 2, 1, 3)).reshape(SEQ, KV_HEADS, HEAD_DIM)
        old_values = jnp.transpose(stored[..., HEAD_DIM:], (0, 2, 1, 3)).reshape(SEQ, KV_HEADS, HEAD_DIM)
        row_ids = jnp.arange(ROWS, dtype=jnp.int32)
        target = jnp.where(row_ids < live_count, positions, SEQ).astype(jnp.int32)
        all_keys = old_keys.at[target].set(new_keys, mode='drop')
        all_values = old_values.at[target].set(new_values, mode='drop')
        allowed = jnp.arange(SEQ, dtype=jnp.int32)[None, :] <= positions[:, None]
        outputs = []
        for kv_head in range(KV_HEADS):
            head_queries = queries[:, kv_head * group_size:(kv_head + 1) * group_size].astype(jnp.float32)
            head_keys = all_keys[:, kv_head].astype(jnp.float32)
            head_values = all_values[:, kv_head].astype(jnp.float32)
            scores = jnp.einsum('rgd,sd->grs', head_queries, head_keys)
            scores = jnp.where(allowed[None], scores, -jnp.inf)
            row_max = lax.optimization_barrier(jnp.max(scores, axis=-1, keepdims=True))
            shifted = jnp.exp(scores - row_max)
            weight = (shifted / lax.optimization_barrier(jnp.sum(shifted, axis=-1, keepdims=True))).astype(jnp.bfloat16)
            outputs.append(jnp.einsum('grs,sd->rgd', weight.astype(jnp.float32), head_values))
        context = jnp.concatenate(outputs, axis=1)
        row_live = (row_ids < live_count)[:, None, None]
        context = jnp.where(row_live, context, 0.0)
        return context.reshape(ROWS, HEADS * HEAD_DIM).astype(jnp.bfloat16)
    return lax.map(one_prompt, (hidden, passage_ids, select_index, select_count))
```

```python
import functools

import jax
import jax.numpy as jnp
from jax import lax
from jax.experimental import pallas as pl
from jax.experimental.pallas import tpu as pltpu
from jax.sharding import PartitionSpec as P

KV_HEADS = 4
HEAD_DIM = 128
ROPE_BASE = 1000000.0
EPSILON = 1e-06
LOG2_E = 1.4426950408889634
MASKED = -1e30


def divisor(total, step, most):
    best = step
    for size in range(step, min(total, most) + 1, step):
        if total % size == 0:
            best = size
    return best if total % best == 0 else total


def tables(positions, scale):
    half_dim = HEAD_DIM // 2
    frequency = ROPE_BASE ** (-(jnp.arange(half_dim, dtype=jnp.float32) * 2.0) / HEAD_DIM)
    angles = positions.astype(jnp.float32)[..., None] * frequency
    cosine = jnp.cos(angles) * scale
    sine = jnp.sin(angles) * scale
    return jnp.concatenate([cosine, cosine], -1), jnp.concatenate([-sine, sine], -1)


def turned(vectors, cosine, sine):
    half_dim = HEAD_DIM // 2
    swapped = jnp.concatenate([vectors[..., half_dim:], vectors[..., :half_dim]], -1)
    return vectors * cosine + swapped * sine


def attend_kernel(
    heads, width, span, scalars, place, sums, cosine, sine, column, keys, values, out, queries
):
    first = scalars[0] + pl.program_id(0) * width
    live = jnp.clip(scalars[1] - first, 0, width)

    @pl.when(live == 0)
    def _():
        out[...] = jnp.zeros_like(out)

    @pl.when(live > 0)
    def _():
        for head in range(heads):
            part = sums[:, head * HEAD_DIM : (head + 1) * HEAD_DIM]
            spun = part * cosine[...] + pltpu.roll(part, HEAD_DIM // 2, 1) * sine[...]
            queries[head * width : (head + 1) * width, :] = spun.astype(jnp.bfloat16)
        lowest = place[first]
        highest = place[first + live - 1]
        limit = jnp.concatenate([column[...]] * heads, axis=0)

        def step(index, carry, masked):
            total, top, mass = carry
            start = pl.multiple_of(index * span, span)
            scores = lax.dot_general(
                queries[...],
                keys[pl.ds(start, span), :],
                (((1,), (1,)), ((), ())),
                preferred_element_type=jnp.float32,
            )
            if masked:
                offset = lax.broadcasted_iota(jnp.int32, scores.shape, 1)
                scores = jnp.where(offset <= limit - start, scores, MASKED)
            peak = jnp.maximum(top, jnp.max(scores, axis=1, keepdims=True))
            weight = jnp.exp2(scores - peak)
            shrink = jnp.exp2(top - peak)
            mass = mass * shrink + jnp.sum(weight, axis=1, keepdims=True)
            total = total * shrink + jnp.dot(
                weight.astype(jnp.bfloat16),
                values[pl.ds(start, span), :],
                preferred_element_type=jnp.float32,
            )
            return total, peak, mass

        carry = (
            jnp.zeros((heads * width, HEAD_DIM), jnp.float32),
            jnp.full((heads * width, 1), MASKED, jnp.float32),
            jnp.zeros((heads * width, 1), jnp.float32),
        )
        clear = (lowest + 1) // span
        carry = lax.fori_loop(0, clear, functools.partial(step, masked=False), carry)
        carry = lax.fori_loop(
            clear, highest // span + 1, functools.partial(step, masked=True), carry
        )
        total, _, mass = carry
        result = total / mass
        row = lax.broadcasted_iota(jnp.int32, (width, HEAD_DIM), 0)
        for head in range(heads):
            part = result[head * width : (head + 1) * width, :]
            out[:, head * HEAD_DIM : (head + 1) * HEAD_DIM] = jnp.where(
                row < live, part, 0.0
            ).astype(out.dtype)


def attend(sums, cosine, sine, positions, first, live_count, keys, values):
    rows, total_width = sums.shape
    heads = total_width // HEAD_DIM
    width = divisor(rows, 16, 48)
    length = keys.shape[0]
    span = divisor(length, 128, 512)
    scalars = jnp.stack([jnp.int32(first), live_count])
    whole = lambda i, *_: (0, 0)
    block = lambda i, *_: (i, 0)
    return pl.pallas_call(
        functools.partial(attend_kernel, heads, width, span),
        out_shape=jax.ShapeDtypeStruct(sums.shape, jnp.bfloat16),
        grid_spec=pltpu.PrefetchScalarGridSpec(
            num_scalar_prefetch=2,
            grid=(rows // width,),
            in_specs=[
                pl.BlockSpec((width, total_width), block),
                pl.BlockSpec((width, HEAD_DIM), block),
                pl.BlockSpec((width, HEAD_DIM), block),
                pl.BlockSpec((width, 1), block),
                pl.BlockSpec((length, HEAD_DIM), whole),
                pl.BlockSpec((length, HEAD_DIM), whole),
            ],
            out_specs=pl.BlockSpec((width, total_width), block),
            scratch_shapes=[pltpu.VMEM((heads * width, HEAD_DIM), jnp.bfloat16)],
        ),
        cost_estimate=pl.CostEstimate(
            flops=2 * rows * total_width * length,
            bytes_accessed=rows * total_width * 6 + length * HEAD_DIM * 4,
            transcendentals=rows * heads * length // 2,
        ),
    )(
        scalars,
        positions,
        sums,
        cosine[first : first + rows],
        sine[first : first + rows],
        positions[first : first + rows, None],
        keys,
        values,
    )


def fetch_passages(passage_cache, passage_ids, kv_head):
    store_rank = lax.axis_index("store")
    pool_dev, _, passage, _ = passage_cache.shape
    head_cache = lax.dynamic_index_in_dim(passage_cache, kv_head, 1, keepdims=False)
    owners = passage_ids // pool_dev
    local_index = passage_ids % pool_dev
    matches = owners == store_rank
    local_slot = jnp.sum(jnp.where(matches, local_index, 0), axis=1)
    present = jnp.any(matches, axis=1)
    outgoing = jnp.take(head_cache, local_slot, axis=0) * present[:, None, None].astype(
        jnp.bfloat16
    )
    incoming = lax.all_to_all(outgoing, "store", split_axis=0, concat_axis=0, tiled=True)
    my_owners = lax.dynamic_index_in_dim(owners, store_rank, 0, keepdims=False)
    fetched = jnp.take(incoming, my_owners, axis=0)
    passages = passage_ids.shape[1]
    cosine, sine = tables(jnp.arange(passages) * passage, 1.0)
    old_keys = turned(
        fetched[..., :HEAD_DIM].astype(jnp.float32), cosine[:, None], sine[:, None]
    ).astype(jnp.bfloat16)
    length = passages * passage
    return old_keys.reshape(length, HEAD_DIM), fetched[..., HEAD_DIM:].reshape(length, HEAD_DIM)


def blend(old_keys, old_values, head_kv, inverse_rms, positions, live_count):
    row_count = positions.shape[0]
    cosine, sine = tables(positions, inverse_rms[:, None])
    new_keys = turned(head_kv[:, :HEAD_DIM], cosine, sine).astype(jnp.bfloat16)
    new_values = (head_kv[:, HEAD_DIM:] * inverse_rms[:, None]).astype(jnp.bfloat16)
    row_ids = jnp.arange(row_count, dtype=jnp.int32)
    target = jnp.where(row_ids < live_count, positions, old_keys.shape[0])
    keys = old_keys.at[target].set(new_keys, mode="drop")
    values = old_values.at[target].set(new_values, mode="drop")
    return keys, values


def gathered(hidden, w_query, w_keyvalue, kv_head):
    partial_kv = jnp.dot(hidden, w_keyvalue, preferred_element_type=jnp.float32)
    proj_kv = lax.psum(partial_kv, "tp")
    head_kv = lax.dynamic_slice_in_dim(proj_kv, kv_head * 2 * HEAD_DIM, 2 * HEAD_DIM, 1)
    tokens = lax.all_gather(hidden, "tp", axis=1, tiled=True)
    widened = tokens.astype(jnp.float32)
    squares = jnp.sum(widened * widened, axis=-1)
    sums = jnp.dot(tokens, w_query, preferred_element_type=jnp.float32)
    return sums, head_kv, squares


def local(hidden, w_query, w_keyvalue, passage_cache, passage_ids, select_index, select_count):
    hidden = hidden[0]
    tp_count = lax.axis_size("tp")
    features = tp_count * hidden.shape[1]
    kv_head = lax.axis_index("tp") // (tp_count // KV_HEADS)
    positions = select_index[0]
    live_count = select_count[0]
    old_keys, old_values = fetch_passages(passage_cache, passage_ids, kv_head)
    sums, head_kv, squares = gathered(hidden, w_query, w_keyvalue, kv_head)
    inverse_rms = lax.rsqrt(squares / features + EPSILON)
    keys, values = blend(old_keys, old_values, head_kv, inverse_rms, positions, live_count)
    cosine, sine = tables(positions, (inverse_rms * (HEAD_DIM**-0.5 * LOG2_E))[:, None])
    context = attend(sums, cosine, sine, positions, 0, live_count, keys, values)
    return context[None]


def solution(mesh):
    in_specs = (
        P("store", None, "tp"),
        P(None, "tp"),
        P("tp", None),
        P("store", None, None, None),
        P(),
        P("store", None),
        P("store"),
    )
    out_specs = P("store", None, "tp")
    return jax.shard_map(local, mesh=mesh, in_specs=in_specs, out_specs=out_specs, check_vma=False)
```

```python
import functools

import jax
import jax.numpy as jnp
from jax import lax
from jax.experimental import pallas as pl
from jax.experimental.pallas import tpu as pltpu
from jax.sharding import PartitionSpec as P

KV_HEADS = 4
HEAD_DIM = 128
ROPE_BASE = 1000000.0
EPSILON = 1e-06
LOG2_E = 1.4426950408889634
MASKED = -1e30
CHUNKS = (4, 4, 3, 1)


def divisor(total, step, most):
    best = step
    for size in range(step, min(total, most) + 1, step):
        if total % size == 0:
            best = size
    return best if total % best == 0 else total


def tables(positions, scale):
    half_dim = HEAD_DIM // 2
    frequency = ROPE_BASE ** (-(jnp.arange(half_dim, dtype=jnp.float32) * 2.0) / HEAD_DIM)
    angles = positions.astype(jnp.float32)[..., None] * frequency
    cosine = jnp.cos(angles) * scale
    sine = jnp.sin(angles) * scale
    return jnp.concatenate([cosine, cosine], -1), jnp.concatenate([-sine, sine], -1)


def turned(vectors, cosine, sine):
    half_dim = HEAD_DIM // 2
    swapped = jnp.concatenate([vectors[..., half_dim:], vectors[..., :half_dim]], -1)
    return vectors * cosine + swapped * sine


def attend_kernel(
    heads, width, span, scalars, place, sums, extra, cosine, sine, column, keys, values, out, queries
):
    first = scalars[0] + pl.program_id(0) * width
    live = jnp.clip(scalars[1] - first, 0, width)

    @pl.when(live == 0)
    def _():
        out[...] = jnp.zeros_like(out)

    @pl.when(live > 0)
    def _():
        for head in range(heads):
            lanes = slice(head * HEAD_DIM, (head + 1) * HEAD_DIM)
            part = sums[:, lanes] + extra[:, lanes].astype(jnp.float32)
            spun = part * cosine[...] + pltpu.roll(part, HEAD_DIM // 2, 1) * sine[...]
            queries[head * width : (head + 1) * width, :] = spun.astype(jnp.bfloat16)
        lowest = place[first]
        highest = place[first + live - 1]
        limit = jnp.concatenate([column[...]] * heads, axis=0)

        def step(index, carry, masked):
            total, top, mass = carry
            start = pl.multiple_of(index * span, span)
            scores = lax.dot_general(
                queries[...],
                keys[pl.ds(start, span), :],
                (((1,), (1,)), ((), ())),
                preferred_element_type=jnp.float32,
            )
            if masked:
                offset = lax.broadcasted_iota(jnp.int32, scores.shape, 1)
                scores = jnp.where(offset <= limit - start, scores, MASKED)
            peak = jnp.maximum(top, jnp.max(scores, axis=1, keepdims=True))
            weight = jnp.exp2(scores - peak)
            shrink = jnp.exp2(top - peak)
            mass = mass * shrink + jnp.sum(weight, axis=1, keepdims=True)
            total = total * shrink + jnp.dot(
                weight.astype(jnp.bfloat16),
                values[pl.ds(start, span), :],
                preferred_element_type=jnp.float32,
            )
            return total, peak, mass

        carry = (
            jnp.zeros((heads * width, HEAD_DIM), jnp.float32),
            jnp.full((heads * width, 1), MASKED, jnp.float32),
            jnp.zeros((heads * width, 1), jnp.float32),
        )
        clear = (lowest + 1) // span
        carry = lax.fori_loop(0, clear, functools.partial(step, masked=False), carry)
        carry = lax.fori_loop(
            clear, highest // span + 1, functools.partial(step, masked=True), carry
        )
        total, _, mass = carry
        result = total / mass
        row = lax.broadcasted_iota(jnp.int32, (width, HEAD_DIM), 0)
        for head in range(heads):
            part = result[head * width : (head + 1) * width, :]
            out[:, head * HEAD_DIM : (head + 1) * HEAD_DIM] = jnp.where(
                row < live, part, 0.0
            ).astype(out.dtype)


def attend(sums, extra, cosine, sine, positions, first, live_count, keys, values):
    rows, total_width = sums.shape
    heads = total_width // HEAD_DIM
    width = divisor(rows, 16, 48)
    length = keys.shape[0]
    span = divisor(length, 128, 512)
    scalars = jnp.stack([jnp.int32(first), live_count])
    whole = lambda i, *_: (0, 0)
    block = lambda i, *_: (i, 0)
    return pl.pallas_call(
        functools.partial(attend_kernel, heads, width, span),
        out_shape=jax.ShapeDtypeStruct(sums.shape, jnp.bfloat16),
        grid_spec=pltpu.PrefetchScalarGridSpec(
            num_scalar_prefetch=2,
            grid=(rows // width,),
            in_specs=[
                pl.BlockSpec((width, total_width), block),
                pl.BlockSpec((width, total_width), block),
                pl.BlockSpec((width, HEAD_DIM), block),
                pl.BlockSpec((width, HEAD_DIM), block),
                pl.BlockSpec((width, 1), block),
                pl.BlockSpec((length, HEAD_DIM), whole),
                pl.BlockSpec((length, HEAD_DIM), whole),
            ],
            out_specs=pl.BlockSpec((width, total_width), block),
            scratch_shapes=[pltpu.VMEM((heads * width, HEAD_DIM), jnp.bfloat16)],
        ),
        cost_estimate=pl.CostEstimate(
            flops=2 * rows * total_width * length,
            bytes_accessed=rows * total_width * 6 + length * HEAD_DIM * 4,
            transcendentals=rows * heads * length // 2,
        ),
    )(
        scalars,
        positions,
        sums,
        extra,
        cosine[first : first + rows],
        sine[first : first + rows],
        positions[first : first + rows, None],
        keys,
        values,
    )


def fetch_passages(passage_cache, passage_ids, kv_head):
    store_rank = lax.axis_index("store")
    pool_dev, _, passage, _ = passage_cache.shape
    head_cache = lax.dynamic_index_in_dim(passage_cache, kv_head, 1, keepdims=False)
    owners = passage_ids // pool_dev
    local_index = passage_ids % pool_dev
    matches = owners == store_rank
    local_slot = jnp.sum(jnp.where(matches, local_index, 0), axis=1)
    present = jnp.any(matches, axis=1)
    outgoing = jnp.take(head_cache, local_slot, axis=0) * present[:, None, None].astype(
        jnp.bfloat16
    )
    incoming = lax.all_to_all(outgoing, "store", split_axis=0, concat_axis=0, tiled=True)
    my_owners = lax.dynamic_index_in_dim(owners, store_rank, 0, keepdims=False)
    fetched = jnp.take(incoming, my_owners, axis=0)
    passages = passage_ids.shape[1]
    cosine, sine = tables(jnp.arange(passages) * passage, 1.0)
    old_keys = turned(
        fetched[..., :HEAD_DIM].astype(jnp.float32), cosine[:, None], sine[:, None]
    ).astype(jnp.bfloat16)
    length = passages * passage
    return old_keys.reshape(length, HEAD_DIM), fetched[..., HEAD_DIM:].reshape(length, HEAD_DIM)


def blend(old_keys, old_values, head_kv, inverse_rms, positions, live_count):
    row_count = positions.shape[0]
    cosine, sine = tables(positions, inverse_rms[:, None])
    new_keys = turned(head_kv[:, :HEAD_DIM], cosine, sine).astype(jnp.bfloat16)
    new_values = (head_kv[:, HEAD_DIM:] * inverse_rms[:, None]).astype(jnp.bfloat16)
    row_ids = jnp.arange(row_count, dtype=jnp.int32)
    target = jnp.where(row_ids < live_count, positions, old_keys.shape[0])
    keys = old_keys.at[target].set(new_keys, mode="drop")
    values = old_values.at[target].set(new_values, mode="drop")
    return keys, values


def product_kernel(steps, step_rows, count, table, *refs):
    sources = refs[:count]
    weights = refs[count : 2 * count]
    out, total = refs[-2:]
    step = pl.program_id(0)

    @pl.when(step == 0)
    def _():
        if len(refs) == 2 * count + 3:
            total[...] = refs[2 * count][...]
        else:
            total[...] = jnp.zeros_like(total)

    width = weights[0].shape[-1]
    parts = out.shape[1] // width
    for index in range(count):
        inside = (step // steps == index) & (table[0, index] > 0)
        place = lax.rem(step, steps)
        column = pl.multiple_of(place // parts * step_rows, step_rows)
        for part in range(parts):

            @pl.when(inside & (lax.rem(place, parts) == part))
            def _():
                total[:, part * width : (part + 1) * width] += jnp.dot(
                    sources[index][:, pl.ds(column, step_rows)],
                    weights[index][...],
                    preferred_element_type=jnp.float32,
                )

    @pl.when(step == pl.num_programs(0) - 1)
    def _():
        out[...] = total[...].astype(out.dtype)


def add_products(base, sources, weights, active, order, step_rows, width, kind):
    rows, depth = sources[0].shape
    count = len(sources)
    extra = () if base is None else (base,)
    block_width = weights[0].shape[1]
    steps = depth // step_rows * (width // block_width)
    still = jnp.where(active[:, None] > 0, order, order[:, :1])
    table = jnp.concatenate([active[None], still.T], 0)

    def weight_map(index):
        def place(step, table_ref):
            at = jnp.clip(step - index * steps, 0, steps - 1)
            return table_ref[1 + at, index], 0

        return place

    whole = lambda step, table_ref: (0, 0)
    return pl.pallas_call(
        functools.partial(product_kernel, steps, step_rows, count),
        out_shape=jax.ShapeDtypeStruct((rows, width), kind),
        grid_spec=pltpu.PrefetchScalarGridSpec(
            num_scalar_prefetch=1,
            grid=(count * steps,),
            in_specs=[pl.BlockSpec((rows, depth), whole, pipeline_mode=pl.Buffered(1))] * count
            + [pl.BlockSpec((step_rows, block_width), weight_map(i)) for i in range(count)]
            + [pl.BlockSpec((rows, width), whole, pipeline_mode=pl.Buffered(1))] * len(extra),
            out_specs=pl.BlockSpec((rows, width), whole),
            scratch_shapes=[pltpu.VMEM((rows, width), jnp.float32)],
        ),
        cost_estimate=pl.CostEstimate(
            flops=2 * rows * depth * width * count,
            bytes_accessed=count * depth * width * 2 + rows * width * 8,
            transcendentals=0,
        ),
    )(table, *sources, *weights, *extra)


def row_chunks(row_count):
    unit = divisor(row_count, 16, 48)
    units = row_count // unit
    shares = CHUNKS if units == sum(CHUNKS) else (units,)
    chunks, end = [], row_count
    for share in shares:
        chunks.append((end - share * unit, share * unit))
        end -= share * unit
    return chunks


def send(value, axis, pairs, name):
    with jax.named_scope(name):
        return lax.ppermute(value, axis, pairs)


def spread(piece, name):
    store_count = lax.axis_size("store")
    swap = lambda value, mask, tag: send(
        value, "store", [(i, i ^ mask) for i in range(store_count)], name + tag
    )
    half = piece.shape[1] // 2
    left, right = piece[None, :, :half], piece[None, :, half:]
    left2 = jnp.concatenate([left, swap(left, 2, "_a2")])
    right2 = jnp.concatenate([right, swap(right, 4, "_b4")])
    left4 = jnp.concatenate([left2, swap(left2, 4, "_a4")])
    right4 = jnp.concatenate([right2, swap(right2, 2, "_b2")])
    mine = jnp.concatenate([left4, right4])
    both = jnp.concatenate([mine, swap(mine, 1, "_c")])
    return both.reshape(-1, half)


def spread_order():
    store_rank = lax.axis_index("store")
    store_count = lax.axis_size("store")
    offset = jnp.arange(store_count, dtype=jnp.int32) ^ store_rank
    core, low, high = offset & 1, (offset >> 1) & 1, (offset >> 2) & 1
    left = core * store_count + low + 2 * high
    right = core * store_count + store_count // 2 + high + 2 * low
    return jnp.stack([left, right], 1).reshape(-1)


def key_value_sums(part, rank):
    last = lax.axis_size("tp") - 1
    size = 2 * HEAD_DIM
    narrow = lambda value: value.astype(jnp.bfloat16)
    passed = None
    own = lax.dynamic_slice_in_dim(part, rank * size, size, 1)
    for step in range(last):
        up = part[:, (step + 1) * size :]
        down = part[:, : (last - step) * size]
        if passed is not None:
            up = up + passed[:, size:]
            down = down + passed[:, :-size]
        from_low = rank == step
        payload = narrow(jnp.where(from_low, up, down))
        pairs = [(step, step + 1), (last - step, last - step - 1)]
        passed = send(payload, "tp", pairs, f"kv{step}").astype(jnp.float32)
        arrived_up = jnp.where(rank == step + 1, passed[:, :size], 0.0)
        arrived_down = jnp.where(rank == last - step - 1, passed[:, -size:], 0.0)
        own = own + arrived_up + arrived_down
    return own


def line(hidden, w_query, w_keyvalue):
    rank = lax.axis_index("tp")
    store_rank = lax.axis_index("store")
    store_count = lax.axis_size("store")
    tp_count = lax.axis_size("tp")
    last = tp_count - 1
    rows, depth = hidden.shape
    width = w_query.shape[1]
    chunks = row_chunks(rows)
    f32, bf16, i32 = jnp.float32, jnp.bfloat16, jnp.int32
    up = [(t, t + 1) for t in range(last)]
    down = [(t + 1, t) for t in range(last)]

    piece_rows = depth // store_count
    near = jnp.where(rank == 0, 2, 1) * depth + store_rank * piece_rows
    far = jnp.where(rank == 0, 3, 0) * depth + store_rank * piece_rows
    helped = []
    for start, name in ((near, "near"), (far, "far")):
        piece = lax.dynamic_slice_in_dim(w_query, start, piece_rows, 0)
        helped.append(send(piece, "tp", [(0, 1), (last, last - 1)], name + "_z"))

    own = [hidden[a : a + n] for a, n in chunks]
    above = [send(x, "tp", up, f"up1_{c}") for c, x in enumerate(own)]
    below = [send(x, "tp", down, f"down1_{c}") for c, x in enumerate(own)]
    above2 = [send(x, "tp", [(1, 2)], f"up2_{c}") for c, x in enumerate(above)]
    below2 = [send(x, "tp", [(2, 1)], f"down2_{c}") for c, x in enumerate(below)]

    part = jnp.dot(hidden, w_keyvalue, preferred_element_type=f32)
    head_kv = key_value_sums(part, rank)
    widened = hidden.astype(f32)
    square = jnp.sum(widened * widened, axis=-1)
    squares = square
    for hop in range(1, tp_count):
        ring = [(t, (t + hop) % tp_count) for t in range(tp_count)]
        squares = squares + send(square, "tp", ring, f"square{hop}")

    near_w, far_w = spread(helped[0], "near"), spread(helped[1], "far")
    helper_order = spread_order()
    step_rows = divisor(depth, 128, 512)
    steps = depth // step_rows
    span = jnp.arange(steps, dtype=i32)
    shard = lambda t: jnp.clip(t, 0, last) * steps + span
    flag = lambda *tests: jnp.stack([jnp.asarray(t).astype(i32) for t in tests])
    first_order = jnp.stack([shard(rank), shard(rank - 1), shard(rank + 1)])
    second_order = jnp.stack([shard(rank + 2), shard(rank - 2)])
    third_order = jnp.stack([helper_order, helper_order])
    inner = flag(rank == 1, rank == 2)

    results = []
    for c in range(len(chunks)):
        near_sums = add_products(
            None, [below[c], above[c]], [near_w, near_w], inner, third_order, piece_rows, width, f32
        )
        far_sums = add_products(
            near_sums,
            [below2[c], above2[c]],
            [far_w, far_w],
            inner,
            third_order,
            piece_rows,
            width,
            bf16,
        )
        extra = send(far_sums, "tp", [(1, 0), (last - 1, last)], f"help_{c}")
        sums = add_products(
            None,
            [own[c], above[c], below[c]],
            [w_query] * 3,
            flag(rank >= 0, rank > 0, rank < last),
            first_order,
            step_rows,
            width,
            f32,
        )
        sums = add_products(
            sums, [below2[c], above2[c]], [w_query] * 2, inner, second_order, step_rows, width, f32
        )
        results.append((sums, extra))
    return results, head_kv, squares


def gathered(hidden, w_query, w_keyvalue, kv_head):
    partial_kv = jnp.dot(hidden, w_keyvalue, preferred_element_type=jnp.float32)
    proj_kv = lax.psum(partial_kv, "tp")
    head_kv = lax.dynamic_slice_in_dim(proj_kv, kv_head * 2 * HEAD_DIM, 2 * HEAD_DIM, 1)
    tokens = lax.all_gather(hidden, "tp", axis=1, tiled=True)
    widened = tokens.astype(jnp.float32)
    squares = jnp.sum(widened * widened, axis=-1)
    sums = jnp.dot(tokens, w_query, preferred_element_type=jnp.float32)
    return sums, head_kv, squares


def local(hidden, w_query, w_keyvalue, passage_cache, passage_ids, select_index, select_count):
    hidden = hidden[0]
    tp_count = lax.axis_size("tp")
    features = tp_count * hidden.shape[1]
    kv_head = lax.axis_index("tp") // (tp_count // KV_HEADS)
    positions = select_index[0]
    live_count = select_count[0]
    old_keys, old_values = fetch_passages(passage_cache, passage_ids, kv_head)
    if tp_count == 4 and KV_HEADS == 4 and lax.axis_size("store") == 8:
        results, head_kv, squares = line(hidden, w_query, w_keyvalue)
        chunks = row_chunks(hidden.shape[0])
    else:
        sums, head_kv, squares = gathered(hidden, w_query, w_keyvalue, kv_head)
        results = [(sums, jnp.zeros(sums.shape, jnp.bfloat16))]
        chunks = [(0, hidden.shape[0])]
    inverse_rms = lax.rsqrt(squares / features + EPSILON)
    keys, values = blend(old_keys, old_values, head_kv, inverse_rms, positions, live_count)
    cosine, sine = tables(positions, (inverse_rms * (HEAD_DIM**-0.5 * LOG2_E))[:, None])
    parts = [
        attend(sums, extra, cosine, sine, positions, first, live_count, keys, values)
        for (sums, extra), (first, _) in zip(results, chunks)
    ]
    context = jnp.concatenate(parts[::-1], axis=0)
    return context[None]


def solution(mesh):
    in_specs = (
        P("store", None, "tp"),
        P(None, "tp"),
        P("tp", None),
        P("store", None, None, None),
        P(),
        P("store", None),
        P("store"),
    )
    out_specs = P("store", None, "tp")
    return jax.shard_map(local, mesh=mesh, in_specs=in_specs, out_specs=out_specs, check_vma=False)
```
